32 devices in a mesh: groups: 2 (over y), fsdp: 8 (over z, x), tensor: 2 (over core).
Axes of the slice: x: 2, y: 2, z: 4, core: 2. Of those that a mesh axis runs over, the one named last changes fastest.
Arguments:
- hidden_states: bfloat16 [8192, 4096], P(('groups', 'fsdp', 'tensor')), parts along dimension 0, may hold values from -6 to 6
- teacher_weight: bfloat16 [4096, 512], P('fsdp', 'tensor'), may hold values from -0.09375 to 0.09375
- student_weight: float32 [8192, 512], P(('groups', 'fsdp'), 'tensor'), parts along dimension 0, may hold values from -1 to 1
- first_moment: float32 [8192, 512], P(('groups', 'fsdp'), 'tensor'), parts along dimension 0, may hold values from -0.06 to 0.06
- second_moment: float32 [8192, 512], P(('groups', 'fsdp'), 'tensor'), parts along dimension 0, may hold values from 1e-05 to 0.001
Outputs:
- new_student: float32 [8192, 512], P(('groups', 'fsdp'), 'tensor'), parts along dimension 0
- new_first: float32 [8192, 512], P(('groups', 'fsdp'), 'tensor'), parts along dimension 0
- new_second: float32 [8192, 512], P(('groups', 'fsdp'), 'tensor'), parts along dimension 0
- distill_loss: float32 [2], P('groups'), parts along dimension 0
The draws below stay inside these ranges and needn't reach their ends.
There are 2 independent parts, one for each index of `groups`. The reference program is written for one: setup_inputs(seed, part) draws one part's arguments, and reference() takes and returns one part's arrays. A program takes and returns all parts, laid end to end along the dimension named above; an argument that names none is the same for every part. Nothing has to cross between parts.
All inputs are finite; a program needn't handle non-finite values.
Results may differ from the reference program's by a relative error of at most 0.0031.
Values may be sent and summed in bfloat16 or wider, within the bound.
No kernel may reach another device: no remote copies, remote signals or barrier semaphores. Data moves between devices by JAX's collectives and lax.ppermute only.
A program may use at most 64 MiB of HBM per device.

```python
import math
import jax
import jax.numpy as jnp
from jax import lax

D = 4096
KV = 512
TOKENS = 4096


def draw_student_weight(key, part):
    key_base = jax.random.fold_in(key, 11)
    key_rows = jax.random.fold_in(key, 12)
    key_cols = jax.random.fold_in(key, 13)
    base = jnp.clip(jax.random.normal(key_base, (D, KV), jnp.float32), -5.0, 5.0)
    row_gain = jnp.exp(jax.random.uniform(key_rows, (D, 1), jnp.float32, 0.0, math.log(10.0)))
    col_gain = jnp.exp(jax.random.uniform(key_cols, (1, KV), jnp.float32, 0.0, math.log(10.0)))
    return base * row_gain * col_gain / (21.5 * math.sqrt(D))


def levels(key, dims, split, smallest, largest):
    factor_of, own = 1.0, jax.random.fold_in(key, 6)
    for position, shards_of in split:
        steps = jnp.exp(jax.random.uniform(jax.random.fold_in(own, position), (shards_of,), jnp.float32, smallest / len(split), largest / len(split)))
        factor_of = factor_of * jnp.repeat(steps, dims[position] // shards_of).reshape([-1 if axis == position else 1 for axis in range(len(dims))])
    return factor_of


def noise(stream_key, dims, scale, reach, split=(), held_as=jnp.bfloat16):
    entries = jax.random.normal(stream_key, dims, jnp.float32) * scale
    if len(split) > 0:
        entries = levels(stream_key, dims, split, -0.22, 0.18) * entries
    return jnp.clip(entries, min=-reach, max=reach).astype(held_as)


def setup_inputs(seed: int = 0, part: int = 0) -> dict:
    keys = jax.random.split(jax.random.key(seed), 6)
    part_splits = jax.random.split(jax.random.fold_in(keys[5], part), 6)
    hidden_states = noise(part_splits[0], (TOKENS, D), 1.0, 6.0, ((0, 16),))
    teacher_weight = noise(keys[1], (D, KV), D ** -0.5, 0.09375, ((0, 8), (1, 2)))
    student_weight = draw_student_weight(jax.random.fold_in(jax.random.fold_in(keys[5], part), 71), part)
    first_moment = noise(part_splits[3], (D, KV), 0.01, 0.06, ((0, 8), (1, 2)), jnp.float32)
    second_moment = jnp.clip(jnp.exp(math.log(0.001) - 4.6051703 * jax.random.uniform(part_splits[4], (D, KV), jnp.float32) ** levels(part_splits[4], (D, KV), ((0, 8), (1, 2)), -0.2, 0.2)), 9.999999747378752e-06, 0.001)
    return dict(hidden_states=hidden_states, teacher_weight=teacher_weight, student_weight=student_weight, first_moment=first_moment, second_moment=second_moment)


two_pi = 2.0 * math.pi
first_bias = 1.0 - 0.9 ** 20
second_bias = 1.0 - 0.95 ** 20

def soft_quantize(weights, quant_scale):
    scaled = weights / quant_scale
    return (quant_scale * (scaled - jnp.sin(two_pi * scaled) / two_pi)).astype(jnp.bfloat16)

def reference(hidden_states, teacher_weight, student_weight, first_moment, second_moment):
    quant_scale = (lax.optimization_barrier(jnp.max(jnp.abs(student_weight), axis=0, keepdims=True)) + 1e-06) / 7.0
    quantized = soft_quantize(student_weight, quant_scale)
    student_out = jnp.dot(hidden_states, quantized, preferred_element_type=jnp.float32)
    teacher_out = jnp.dot(hidden_states, teacher_weight, preferred_element_type=jnp.float32)
    residual = student_out - teacher_out
    distill_loss = jnp.sum(residual * residual).reshape(1) / TOKENS
    grad_out = (residual * (2.0 / TOKENS)).astype(jnp.bfloat16)
    gradient = lax.dot_general(hidden_states, grad_out, (((0,), (0,)), ((), ())), preferred_element_type=jnp.float32)
    new_first = 0.9 * first_moment + 0.1 * gradient
    new_second = 0.95 * second_moment + 0.05 * gradient * gradient
    update = new_first / first_bias / (jnp.sqrt(new_second / second_bias) + 1e-08)
    new_student = student_weight - 0.001 * (update + 0.1 * student_weight)
    return (new_student, new_first, new_second, distill_loss)
```

```python
import math

import jax
import jax.numpy as jnp
from jax import lax
from jax.experimental import pallas as pl
from jax.experimental.pallas import tpu as pltpu
from jax.sharding import PartitionSpec as P

two_pi = 2.0 * math.pi
first_bias = 1.0 - 0.9**20
second_bias = 1.0 - 0.95**20
f32 = jnp.float32
bf16 = jnp.bfloat16


def soft_quantize(weights, quant_scale):
    scaled = weights / quant_scale
    return (quant_scale * (scaled - jnp.sin(two_pi * scaled) / two_pi)).astype(bf16)


def adamw(gradient, student_weight, first_moment, second_moment):
    new_first = 0.9 * first_moment + 0.1 * gradient
    new_second = 0.95 * second_moment + 0.05 * gradient * gradient
    update = new_first / first_bias / (jnp.sqrt(new_second / second_bias) + 1e-08)
    new_student = student_weight - 0.001 * (update + 0.1 * student_weight)
    return new_student, new_first, new_second


def generic(hidden_states, teacher_weight, student_weight, first_moment, second_moment):
    all_inputs = lax.all_gather(hidden_states, "tensor", axis=0, tiled=True)
    total_tokens = all_inputs.shape[0] * lax.axis_size("fsdp")
    local_max = jnp.max(jnp.abs(student_weight), axis=0, keepdims=True)
    quant_scale = (lax.pmax(local_max, "fsdp") + 1e-06) / 7.0
    quantized = soft_quantize(student_weight, quant_scale)
    difference = (quantized.astype(f32) - teacher_weight.astype(f32)).astype(bf16)
    difference = lax.all_gather(difference, "fsdp", axis=0, tiled=True)
    residual = jnp.dot(all_inputs, difference, preferred_element_type=f32)
    squared = jnp.sum(residual * residual).reshape(1)
    distill_loss = lax.psum(squared, ("fsdp", "tensor")) / total_tokens
    grad_out = (residual * (2.0 / total_tokens)).astype(bf16)
    partial = lax.dot_general(
        all_inputs, grad_out, (((0,), (0,)), ((), ())), preferred_element_type=f32
    )
    gradient = lax.psum_scatter(partial, "fsdp", scatter_dimension=0, tiled=True)
    return (*adamw(gradient, student_weight, first_moment, second_moment), distill_loss)


def vmem(n):
    return [pl.BlockSpec(memory_space=pltpu.VMEM)] * n


params = pltpu.CompilerParams(vmem_limit_bytes=16 * 2**20)


def held(*arrays):
    return [pltpu.with_memory_space_constraint(a, pltpu.VMEM) for a in arrays]


def sort_features(hidden_states, blocks):
    tokens, features = hidden_states.shape
    width = features // (2 * blocks)

    def kernel(h_ref, keep_ref, send_ref):
        index = lax.axis_index("fsdp")
        rank, half = index // 2, index % 2
        for k in range(blocks):
            block = jnp.bitwise_xor(rank, k) * 2
            for ref, which in ((send_ref, 1 - half), (keep_ref, half)):
                start = pl.multiple_of((block + which) * width, width)
                ref[:, k * width : (k + 1) * width] = h_ref[:, pl.ds(start, width)]

    shape = pltpu.VMEM((tokens, features // 2), bf16)
    return pl.pallas_call(
        kernel, out_shape=(shape, shape), in_specs=vmem(1), out_specs=tuple(vmem(2)),
        name="sort_features", compiler_params=params,
    )(*held(hidden_states))


def partial_residual(pieces, differences):
    tokens = pieces[0].shape[0]
    width, columns = differences[0].shape
    n, m = len(pieces), len(differences)

    def kernel(*refs):
        h_refs, d_refs, (wide_ref, sent_ref) = refs[:n], refs[n : n + m], refs[n + m :]
        for i, h_ref in enumerate(h_refs):
            total = jnp.zeros((tokens, columns), f32)
            for k, d_ref in enumerate(d_refs):
                total += jnp.dot(
                    h_ref[:, k * width : (k + 1) * width], d_ref[...],
                    preferred_element_type=f32,
                )
            rows = slice(i * tokens, (i + 1) * tokens)
            wide_ref[rows, :] = total
            sent_ref[rows, :] = total.astype(bf16)

    shape = (n * tokens, columns)
    return pl.pallas_call(
        kernel,
        out_shape=(pltpu.VMEM(shape, f32), pltpu.VMEM(shape, bf16)),
        in_specs=vmem(n + m), out_specs=tuple(vmem(2)), name="partial_residual", compiler_params=params,
    )(*held(*pieces, *differences))


def partial_gradient(pieces, mine, theirs, blocks, total_tokens):
    tokens, features = pieces[0].shape
    width, columns, n = features // blocks, mine.shape[1], len(pieces)

    def kernel(*refs):
        h_refs, mine_ref, theirs_ref = refs[:n], refs[n], refs[n + 1]
        loss_ref, own_ref, *send_refs = refs[n + 2 :]
        half = n * tokens // 2
        top = mine_ref[:half, :] + theirs_ref[half:, :].astype(f32)
        bottom = mine_ref[half:, :] + theirs_ref[:half, :].astype(f32)
        loss_ref[...] = jnp.sum(top * top, axis=0, keepdims=True)
        grad_out = jnp.concatenate([top, bottom], axis=0) * (2.0 / total_tokens)
        grad_out = grad_out.astype(bf16)
        for k in range(blocks - 1, -1, -1):
            total = jnp.zeros((columns, width), f32)
            for i, h_ref in enumerate(h_refs):
                total += lax.dot_general(
                    grad_out[i * tokens : (i + 1) * tokens, :],
                    h_ref[:, k * width : (k + 1) * width],
                    (((0,), (0,)), ((), ())), preferred_element_type=f32,
                )
            if k:
                send_refs[k - 1][...] = total.astype(bf16)
            else:
                own_ref[...] = total

    shape = (columns, width)
    return pl.pallas_call(
        kernel,
        out_shape=(
            pltpu.VMEM((1, columns), f32), pltpu.VMEM(shape, f32),
            *[pltpu.VMEM(shape, bf16)] * (blocks - 1),
        ),
        in_specs=vmem(n + 2), out_specs=tuple(vmem(blocks + 1)), name="partial_gradient", compiler_params=params,
    )(*held(*pieces, mine, theirs))


def apply_update(own, received, student_weight, first_moment, second_moment):
    n = len(received)

    def kernel(own_ref, *refs):
        gradient = own_ref[...]
        for ref in refs[:n]:
            gradient += ref[...].astype(f32)
        w_ref, m_ref, v_ref, *out_refs = refs[n:]
        news = adamw(gradient.T, w_ref[...], m_ref[...], v_ref[...])
        for ref, new in zip(out_refs, news, strict=True):
            ref[...] = new

    shape = jax.ShapeDtypeStruct(student_weight.shape, f32)
    return pl.pallas_call(
        kernel, out_shape=(shape,) * 3, in_specs=vmem(n + 4), out_specs=tuple(vmem(3)),
        name="apply_update", compiler_params=params,
    )(*held(own, *received, student_weight, first_moment, second_moment))


def paired(hidden_states, teacher_weight, student_weight, first_moment, second_moment):
    fsdp = lax.axis_size("fsdp")
    blocks = fsdp // 2
    total_tokens = hidden_states.shape[0] * fsdp * lax.axis_size("tensor")

    def flip(array, bit):
        return lax.ppermute(array, "fsdp", [(i, i ^ bit) for i in range(fsdp)])

    def swap_cores(array):
        return lax.ppermute(array, "tensor", [(0, 1), (1, 0)])

    column_max = jnp.max(jnp.abs(student_weight), axis=0, keepdims=True)
    keep, send = sort_features(hidden_states, blocks)
    column_max = jnp.maximum(column_max, flip(column_max, 1))
    send, column_max = lax.optimization_barrier((send, column_max))
    peer = flip(send, 1)
    bit = 2
    while bit < fsdp:
        column_max = jnp.maximum(column_max, flip(column_max, bit))
        bit *= 2
    quant_scale = (column_max + 1e-06) / 7.0
    quantized = soft_quantize(student_weight, quant_scale)
    difference = (quantized.astype(f32) - teacher_weight.astype(f32)).astype(bf16)
    differences = [difference] + [flip(difference, 2 * k) for k in range(1, blocks)]
    peer, differences = lax.optimization_barrier((peer, differences))
    pieces = [keep, swap_cores(keep), peer, swap_cores(peer)]
    mine, sent = partial_residual(pieces, differences)
    theirs = flip(sent, 1)
    loss, own, *partials = partial_gradient(pieces, mine, theirs, blocks, total_tokens)
    received = [flip(p, 2 * k) for k, p in enumerate(partials, 1)]
    loss = jnp.sum(loss).reshape(1)
    bit = 1
    while bit < fsdp:
        loss = loss + flip(loss, bit)
        bit *= 2
    loss = (loss + swap_cores(loss)) / total_tokens
    news = apply_update(own, received, student_weight, first_moment, second_moment)
    return (*news, loss)


def solution(mesh):
    fsdp, tensor = mesh.shape["fsdp"], mesh.shape["tensor"]

    def per_device(hidden_states, *weights):
        rows = weights[0].shape[0]
        few = fsdp in (4, 8, 16) and tensor == 2 and rows % 128 == 0
        return (paired if few else generic)(hidden_states, *weights)

    rows = P(("groups", "fsdp"), "tensor")
    in_specs = (P(("groups", "fsdp", "tensor"), None), P("fsdp", "tensor"), rows, rows, rows)
    out_specs = (rows, rows, rows, P("groups"))
    return jax.shard_map(
        per_device, mesh=mesh, in_specs=in_specs, out_specs=out_specs, check_vma=False
    )
```

```python
import math

import jax
import jax.numpy as jnp
from jax import lax
from jax.experimental import pallas as pl
from jax.experimental.pallas import tpu as pltpu
from jax.sharding import PartitionSpec as P

two_pi = 2.0 * math.pi
first_bias = 1.0 - 0.9**20
second_bias = 1.0 - 0.95**20
f32 = jnp.float32
bf16 = jnp.bfloat16


def soft_quantize(weights, quant_scale):
    scaled = weights / quant_scale
    return (quant_scale * (scaled - jnp.sin(two_pi * scaled) / two_pi)).astype(bf16)


def adamw(gradient, student_weight, first_moment, second_moment):
    new_first = 0.9 * first_moment + 0.1 * gradient
    new_second = 0.95 * second_moment + 0.05 * gradient * gradient
    update = new_first / first_bias / (jnp.sqrt(new_second / second_bias) + 1e-08)
    new_student = student_weight - 0.001 * (update + 0.1 * student_weight)
    return new_student, new_first, new_second


def generic(hidden_states, teacher_weight, student_weight, first_moment, second_moment):
    all_inputs = lax.all_gather(hidden_states, "tensor", axis=0, tiled=True)
    total_tokens = all_inputs.shape[0] * lax.axis_size("fsdp")
    local_max = jnp.max(jnp.abs(student_weight), axis=0, keepdims=True)
    quant_scale = (lax.pmax(local_max, "fsdp") + 1e-06) / 7.0
    quantized = soft_quantize(student_weight, quant_scale)
    difference = (quantized.astype(f32) - teacher_weight.astype(f32)).astype(bf16)
    difference = lax.all_gather(difference, "fsdp", axis=0, tiled=True)
    residual = jnp.dot(all_inputs, difference, preferred_element_type=f32)
    squared = jnp.sum(residual * residual).reshape(1)
    distill_loss = lax.psum(squared, ("fsdp", "tensor")) / total_tokens
    grad_out = (residual * (2.0 / total_tokens)).astype(bf16)
    partial = lax.dot_general(
        all_inputs, grad_out, (((0,), (0,)), ((), ())), preferred_element_type=f32
    )
    gradient = lax.psum_scatter(partial, "fsdp", scatter_dimension=0, tiled=True)
    return (*adamw(gradient, student_weight, first_moment, second_moment), distill_loss)


params = pltpu.CompilerParams(vmem_limit_bytes=16 * 2**20)
sine_terms = (
    6.579736267281999,
    -12.987878760960296,
    12.208113946775761,
    -6.6937816308195295,
    2.4016117188086827,
    -0.6033682700805688,
    0.1006404612407522,
)


def vmem(n):
    return [pl.BlockSpec(memory_space=pltpu.VMEM)] * n


def held(*arrays):
    return [pltpu.with_memory_space_constraint(a, pltpu.VMEM) for a in arrays]


def rounded(array):
    return lax.reduce_precision(array, 8, 7)


def high_low(array):
    high = rounded(array)
    return high.astype(bf16), (array - high).astype(bf16)


def weight_difference(student_weight, teacher_weight, column_max):
    quant_scale = (column_max + 1e-06) / 7.0
    scaled = student_weight / quant_scale
    whole = jnp.round(scaled)
    rest = scaled - whole
    square = rest * rest
    series = jnp.full_like(square, sine_terms[-1])
    for term in sine_terms[-2::-1]:
        series = series * square + term
    quantized = rounded(quant_scale * (whole + rest * square * series))
    return quantized - teacher_weight.astype(f32)


def sort_features(hidden_states, blocks):
    tokens, features = hidden_states.shape
    width = features // (2 * blocks)

    def kernel(h_ref, keep_ref, send_ref):
        index = lax.axis_index("fsdp")
        rank, half = index // 2, index % 2
        for k in range(blocks):
            block = jnp.bitwise_xor(rank, k) * 2
            where = slice(k * width, (k + 1) * width)
            start = pl.multiple_of((block + half) * width, width)
            keep_ref[:, where] = h_ref[:, pl.ds(start, width)]
            start = pl.multiple_of((block + 1 - half) * width, width)
            send_ref[:, where] = h_ref[:, pl.ds(start, width)]

    shape = pltpu.VMEM((tokens, features // 2), bf16)
    return pl.pallas_call(
        kernel, out_shape=(shape, shape), in_specs=vmem(1), out_specs=tuple(vmem(2)),
        name="sort_features", compiler_params=params,
    )(*held(hidden_states))


def row_starts(pieces):
    starts = [0]
    for piece in pieces:
        starts.append(starts[-1] + piece.shape[0])
    return starts


def partial_residual(pieces, highs, lows):
    starts = row_starts(pieces)
    width, columns = highs[0].shape
    n, m = len(pieces), len(highs)

    def kernel(*refs):
        h_refs, d_refs, (wide_ref, sent_ref) = refs[:n], refs[n : n + 2 * m], refs[n + 2 * m :]
        weights = [
            jnp.concatenate([high[...], low[...]], axis=1)
            for high, low in zip(d_refs[:m], d_refs[m:], strict=True)
        ]
        for i, h_ref in enumerate(h_refs):
            total = jnp.zeros((h_ref.shape[0], 2 * columns), f32)
            for k, weight in enumerate(weights):
                total += jnp.dot(
                    h_ref[:, k * width : (k + 1) * width], weight, preferred_element_type=f32
                )
            total = (total[:, :columns] + total[:, columns:]) * 2.0**-15
            rows = slice(starts[i], starts[i + 1])
            wide_ref[rows, :] = total
            sent_ref[rows, :] = total.astype(bf16)

    shape = (starts[-1], columns)
    return pl.pallas_call(
        kernel,
        out_shape=(pltpu.VMEM(shape, f32), pltpu.VMEM(shape, bf16)),
        in_specs=vmem(n + 2 * m), out_specs=tuple(vmem(2)), name="partial_residual",
        compiler_params=params,
    )(*held(*pieces, *highs, *lows))


def split_float(array):
    rows = []
    for _ in range(3):
        rows.append(array.astype(bf16))
        array = array - rows[-1].astype(f32)
    return rows


note_rows = 16


def write_note(ref, start, row):
    width = ref.shape[1]
    parts = [p.astype(f32) for p in split_float(row)]
    parts.append(jnp.zeros((note_rows - 3, row.shape[1]), f32))
    note = jnp.concatenate(parts, axis=0).astype(bf16)
    pad = jnp.zeros((note_rows, width - row.shape[1]), bf16)
    ref[start : start + note_rows, :] = jnp.concatenate([note, pad], axis=1)


def read_note(ref, start, columns):
    note = ref[start : start + note_rows, :columns].astype(f32)
    return note[0:1, :] + note[1:2, :] + note[2:3, :]


def partial_gradient(pieces, mine, theirs, loss, total_tokens, ride):
    starts, features = row_starts(pieces), pieces[0].shape[1]
    width, columns, n = features // 4, mine.shape[1], len(pieces)

    def kernel(*refs):
        h_refs, mine_ref, theirs_ref, before_ref = refs[:n], *refs[n : n + 3]
        loss_ref, own_ref, far_ref, send_ref, *near_refs = refs[n + 3 :]
        half = starts[-1] // 2
        top, bottom = mine_ref[:half, :], mine_ref[half:, :]
        their_bottom = theirs_ref[:half, :].astype(f32)
        their_top = theirs_ref[half:, :].astype(f32)
        top, bottom = top + their_top, bottom + their_bottom
        grad_out = jnp.concatenate([top, bottom], axis=0) * (2.0 / total_tokens)
        grad_out = grad_out.astype(bf16)
        for k in (3, 1, 2, 0):
            total = jnp.zeros((columns, width), f32)
            for i, h_ref in enumerate(h_refs):
                total += lax.dot_general(
                    grad_out[starts[i] : starts[i + 1], :],
                    h_ref[:, k * width : (k + 1) * width],
                    (((0,), (0,)), ((), ())), preferred_element_type=f32,
                )
            if k == 3:
                send_ref[:columns, :] = total.astype(bf16)
            elif k == 1:
                near = total.astype(bf16)
                if ride:
                    send_ref[columns + note_rows :, :] = near
                else:
                    near_refs[0][...] = near
            elif k == 2:
                far_ref[...] = total
            else:
                own_ref[...] = total
        squares = [
            jnp.sum(jnp.square(a.astype(bf16).astype(f32) + b), axis=0, keepdims=True)
            for a, b in (
                (mine_ref[:half, :], their_top),
                (mine_ref[half:, :], their_bottom),
            )
        ]
        total = before_ref[...] + (squares[0] + squares[1])
        loss_ref[...] = total
        write_note(send_ref, columns, total)

    shape = (columns, width)
    return pl.pallas_call(
        kernel,
        out_shape=(
            pltpu.VMEM((1, columns), f32), pltpu.VMEM(shape, f32), pltpu.VMEM(shape, f32),
            pltpu.VMEM((columns * (1 + ride) + note_rows, width), bf16),
            *[pltpu.VMEM(shape, bf16)] * (1 - ride),
        ),
        in_specs=vmem(n + 3), out_specs=tuple(vmem(5 - ride)), name="partial_gradient",
        compiler_params=params,
    )(*held(*pieces, mine, theirs, loss))


def join_far(far, got, loss):
    columns, width = far.shape

    def kernel(far_ref, got_ref, loss_ref, send_ref, sum_ref):
        total = far_ref[...] + got_ref[:columns, :].astype(f32)
        send_ref[:columns, :] = total.astype(bf16)
        both = loss_ref[...] + read_note(got_ref, columns, columns)
        sum_ref[...] = both
        write_note(send_ref, columns, both)

    return pl.pallas_call(
        kernel,
        out_shape=(pltpu.VMEM((columns + note_rows, width), bf16), pltpu.VMEM((1, columns), f32)),
        in_specs=vmem(3), out_specs=tuple(vmem(2)), name="join_far", compiler_params=params,
    )(*held(far, got, loss))


def total_loss(loss, got):
    columns = loss.shape[1]

    def kernel(loss_ref, got_ref, out_ref):
        out_ref[...] = loss_ref[...] + read_note(got_ref, columns, columns)

    return pl.pallas_call(
        kernel, out_shape=pltpu.VMEM((1, columns), f32), in_specs=vmem(2), out_specs=vmem(1)[0],
        name="total_loss", compiler_params=params,
    )(*held(loss, got))


def apply_update(half, own, near, far, states, news=()):
    width, columns = own.shape[1], own.shape[0]
    n = len(news)

    def kernel(own_ref, near_ref, far_ref, w_ref, m_ref, v_ref, *refs):
        gradient = own_ref[...] + near_ref[-columns:, :].astype(f32)
        gradient += far_ref[:columns, :].astype(f32)
        where = (slice(None), slice(half * columns, (half + 1) * columns))
        results = adamw(gradient.T, w_ref[where], m_ref[where], v_ref[where])
        for ref, result in zip(refs[n:], results, strict=True):
            ref[...] = result

    shape = jax.ShapeDtypeStruct(states[0].shape, f32)
    block = pl.BlockSpec((width, columns), lambda i: (0, half))
    return pl.pallas_call(
        kernel, grid=(1,), out_shape=(shape,) * 3,
        in_specs=vmem(6) + [pl.BlockSpec(memory_space=pl.ANY)] * n, out_specs=(block,) * 3,
        input_output_aliases={6 + i: i for i in range(n)},
        name="apply_update", compiler_params=params,
    )(*held(own, near, far, *states), *news)


def paired(hidden_states, teacher_weight, student_weight, first_moment, second_moment):
    fsdp = lax.axis_size("fsdp")
    blocks = fsdp // 2
    total_tokens = hidden_states.shape[0] * fsdp * lax.axis_size("tensor")
    columns = student_weight.shape[1] // 2
    halves = [slice(0, columns), slice(columns, 2 * columns)]

    def flip(array, bit):
        return lax.ppermute(array, "fsdp", [(i, i ^ bit) for i in range(fsdp)])

    def swap_cores(array):
        return lax.ppermute(array, "tensor", [(0, 1), (1, 0)])

    def together(*values):
        return lax.optimization_barrier(values)

    column_max = jnp.max(jnp.abs(student_weight), axis=0, keepdims=True)
    keep, send = sort_features(hidden_states, blocks)
    column_max = jnp.maximum(column_max, flip(column_max, 1))
    keep, column_max = together(keep, column_max)
    peer = flip(send, 1)
    near_keep = swap_cores(keep)
    column_max = jnp.maximum(column_max, flip(column_max, 2))
    column_max = jnp.maximum(column_max, flip(column_max, 4))
    difference = weight_difference(student_weight, teacher_weight, column_max) * 2.0**15
    coded = difference.astype(jnp.float16)

    far = flip(coded, 4)
    near = flip(coded, 2)
    far, near, peer, near_keep = together(far, near, peer, near_keep)
    across = [flip(far[:, half], 2) for half in halves]
    pieces = [keep, near_keep, peer, swap_cores(peer)]

    def residual(c):
        parts = [p[:, halves[c]].astype(f32) for p in (difference, near, far)]
        pairs = [high_low(p) for p in (*parts, across[c].astype(f32))]
        return partial_residual(pieces, [p[0] for p in pairs], [p[1] for p in pairs])

    mine, sent = residual(0)
    theirs = flip(sent, 1)
    mine_next, sent_next = residual(1)
    theirs_next = flip(sent_next, 1)

    loss = jnp.zeros((1, columns), f32)
    loss, own, rest, to_across, to_near = partial_gradient(
        pieces, mine, theirs, loss, total_tokens, False
    )
    from_across = flip(to_across, 2)
    theirs_next, from_across = together(theirs_next, from_across)
    loss_next, own_next, rest_next, to_across = partial_gradient(
        pieces, mine_next, theirs_next, loss, total_tokens, True
    )
    from_across_next = flip(to_across, 2)
    from_near = flip(to_near, 2)
    to_far, _ = join_far(rest, from_across, loss)
    to_far, from_near = together(to_far, from_near)
    from_far = flip(to_far, 4)
    states = (student_weight, first_moment, second_moment)
    from_across_next, from_far = together(from_across_next, from_far)
    news = apply_update(0, own, from_near, from_far, states)
    to_far, loss = join_far(rest_next, from_across_next, loss_next)
    from_far_next = flip(to_far, 4)
    from_far_next, *news = together(from_far_next, *news)
    loss = total_loss(loss, from_far_next)
    loss = jnp.sum(loss + swap_cores(loss)).reshape(1) / total_tokens
    news = apply_update(1, own_next, from_across_next, from_far_next, states, news)
    return (*news, loss)


def solution(mesh):
    fsdp, tensor = mesh.shape["fsdp"], mesh.shape["tensor"]

    def per_device(hidden_states, *weights):
        rows = weights[0].shape[0]
        few = fsdp == 8 and tensor == 2 and rows % 128 == 0 and weights[0].shape[1] % 256 == 0
        return (paired if few else generic)(hidden_states, *weights)

    rows = P(("groups", "fsdp"), "tensor")
    in_specs = (P(("groups", "fsdp", "tensor"), None), P("fsdp", "tensor"), rows, rows, rows)
    out_specs = (rows, rows, rows, P("groups"))
    return jax.shard_map(
        per_device, mesh=mesh, in_specs=in_specs, out_specs=out_specs, check_vma=False
    )
```

```python
import math

import jax
import jax.numpy as jnp
from jax import lax
from jax.experimental import pallas as pl
from jax.experimental.pallas import tpu as pltpu
from jax.sharding import PartitionSpec as P

two_pi = 2.0 * math.pi
first_bias = 1.0 - 0.9**20
second_bias = 1.0 - 0.95**20
f32 = jnp.float32
bf16 = jnp.bfloat16


def soft_quantize(weights, quant_scale):
    scaled = weights / quant_scale
    return (quant_scale * (scaled - jnp.sin(two_pi * scaled) / two_pi)).astype(bf16)


def adamw(gradient, student_weight, first_moment, second_moment):
    new_first = 0.9 * first_moment + 0.1 * gradient
    new_second = 0.95 * second_moment + 0.05 * gradient * gradient
    update = new_first / first_bias / (jnp.sqrt(new_second / second_bias) + 1e-08)
    new_student = student_weight - 0.001 * (update + 0.1 * student_weight)
    return new_student, new_first, new_second


def generic(hidden_states, teacher_weight, student_weight, first_moment, second_moment):
    all_inputs = lax.all_gather(hidden_states, "tensor", axis=0, tiled=True)
    total_tokens = all_inputs.shape[0] * lax.axis_size("fsdp")
    local_max = jnp.max(jnp.abs(student_weight), axis=0, keepdims=True)
    quant_scale = (lax.pmax(local_max, "fsdp") + 1e-06) / 7.0
    quantized = soft_quantize(student_weight, quant_scale)
    difference = (quantized.astype(f32) - teacher_weight.astype(f32)).astype(bf16)
    difference = lax.all_gather(difference, "fsdp", axis=0, tiled=True)
    residual = jnp.dot(all_inputs, difference, preferred_element_type=f32)
    squared = jnp.sum(residual * residual).reshape(1)
    distill_loss = lax.psum(squared, ("fsdp", "tensor")) / total_tokens
    grad_out = (residual * (2.0 / total_tokens)).astype(bf16)
    partial = lax.dot_general(
        all_inputs, grad_out, (((0,), (0,)), ((), ())), preferred_element_type=f32
    )
    gradient = lax.psum_scatter(partial, "fsdp", scatter_dimension=0, tiled=True)
    return (*adamw(gradient, student_weight, first_moment, second_moment), distill_loss)


params = pltpu.CompilerParams(vmem_limit_bytes=16 * 2**20)
sine_terms = (
    6.579736267281999,
    -12.987878760960296,
    12.208113946775761,
    -6.6937816308195295,
    2.4016117188086827,
    -0.6033682700805688,
    0.1006404612407522,
)


def vmem(n):
    return [pl.BlockSpec(memory_space=pltpu.VMEM)] * n


def held(*arrays):
    return [pltpu.with_memory_space_constraint(a, pltpu.VMEM) for a in arrays]


def rounded(array):
    return lax.reduce_precision(array, 8, 7)


def high_low(array):
    high = rounded(array)
    return high.astype(bf16), (array - high).astype(bf16)


def weight_difference(student_weight, teacher_weight, column_max):
    quant_scale = (column_max + 1e-06) / 7.0
    scaled = student_weight / quant_scale
    whole = jnp.round(scaled)
    rest = scaled - whole
    square = rest * rest
    series = jnp.full_like(square, sine_terms[-1])
    for term in sine_terms[-2::-1]:
        series = series * square + term
    quantized = rounded(quant_scale * (whole + rest * square * series))
    return quantized - teacher_weight.astype(f32)


def sort_features(hidden_states, blocks):
    tokens, features = hidden_states.shape
    width = features // (2 * blocks)

    def kernel(h_ref, keep_ref, send_ref):
        index = lax.axis_index("fsdp")
        rank, half = index // 2, index % 2
        for k in range(blocks):
            block = jnp.bitwise_xor(rank, k) * 2
            where = slice(k * width, (k + 1) * width)
            start = pl.multiple_of((block + half) * width, width)
            keep_ref[:, where] = h_ref[:, pl.ds(start, width)]
            start = pl.multiple_of((block + 1 - half) * width, width)
            send_ref[:, where] = h_ref[:, pl.ds(start, width)]

    shape = pltpu.VMEM((tokens, features // 2), bf16)
    return pl.pallas_call(
        kernel, out_shape=(shape, shape), in_specs=vmem(1), out_specs=tuple(vmem(2)),
        name="sort_features", compiler_params=params,
    )(*held(hidden_states))


def row_starts(pieces):
    starts = [0]
    for piece in pieces:
        starts.append(starts[-1] + piece.shape[0])
    return starts


def partial_residual(pieces, highs, lows):
    starts = row_starts(pieces)
    width, columns = highs[0].shape
    n, m = len(pieces), len(highs)

    def kernel(*refs):
        h_refs, d_refs, (wide_ref, sent_ref) = refs[:n], refs[n : n + 2 * m], refs[n + 2 * m :]
        weights = [
            jnp.concatenate([high[...], low[...]], axis=1)
            for high, low in zip(d_refs[:m], d_refs[m:], strict=True)
        ]
        for i, h_ref in enumerate(h_refs):
            total = jnp.zeros((h_ref.shape[0], 2 * columns), f32)
            for k, weight in enumerate(weights):
                total += jnp.dot(
                    h_ref[:, k * width : (k + 1) * width], weight, preferred_element_type=f32
                )
            total = (total[:, :columns] + total[:, columns:]) * 2.0**-15
            rows = slice(starts[i], starts[i + 1])
            wide_ref[rows, :] = total
            sent_ref[rows, :] = total.astype(bf16)

    shape = (starts[-1], columns)
    return pl.pallas_call(
        kernel,
        out_shape=(pltpu.VMEM(shape, f32), pltpu.VMEM(shape, bf16)),
        in_specs=vmem(n + 2 * m), out_specs=tuple(vmem(2)), name="partial_residual",
        compiler_params=params,
    )(*held(*pieces, *highs, *lows))


def split_float(array):
    rows = []
    for _ in range(3):
        rows.append(array.astype(bf16))
        array = array - rows[-1].astype(f32)
    return rows


note_rows = 16


def write_note(ref, start, row):
    width = ref.shape[1]
    parts = [p.astype(f32) for p in split_float(row)]
    parts.append(jnp.zeros((note_rows - 3, row.shape[1]), f32))
    note = jnp.concatenate(parts, axis=0).astype(bf16)
    pad = jnp.zeros((note_rows, width - row.shape[1]), bf16)
    ref[start : start + note_rows, :] = jnp.concatenate([note, pad], axis=1)


def read_note(ref, start, columns):
    note = ref[start : start + note_rows, :columns].astype(f32)
    return note[0:1, :] + note[1:2, :] + note[2:3, :]


def partial_gradient(pieces, mine, theirs, loss, total_tokens, ride):
    starts, features = row_starts(pieces), pieces[0].shape[1]
    width, columns, n = features // 4, mine.shape[1], len(pieces)

    def kernel(*refs):
        h_refs, mine_ref, theirs_ref, before_ref = refs[:n], *refs[n : n + 3]
        loss_ref, own_ref, far_ref, send_ref, *near_refs = refs[n + 3 :]
        half = starts[-1] // 2
        top, bottom = mine_ref[:half, :], mine_ref[half:, :]
        their_bottom = theirs_ref[:half, :].astype(f32)
        their_top = theirs_ref[half:, :].astype(f32)
        top, bottom = top + their_top, bottom + their_bottom
        grad_out = jnp.concatenate([top, bottom], axis=0) * (2.0 / total_tokens)
        grad_out = grad_out.astype(bf16)
        for k in (3, 1, 2, 0):
            total = jnp.zeros((columns, width), f32)
            for i, h_ref in enumerate(h_refs):
                total += lax.dot_general(
                    grad_out[starts[i] : starts[i + 1], :],
                    h_ref[:, k * width : (k + 1) * width],
                    (((0,), (0,)), ((), ())), preferred_element_type=f32,
                )
            if k == 3:
                send_ref[:columns, :] = total.astype(bf16)
            elif k == 1:
                near = total.astype(bf16)
                if ride:
                    send_ref[columns + note_rows :, :] = near
                else:
                    near_refs[0][...] = near
            elif k == 2:
                far_ref[...] = total
            else:
                own_ref[...] = total
        squares = [
            jnp.sum(jnp.square(a.astype(bf16).astype(f32) + b), axis=0, keepdims=True)
            for a, b in (
                (mine_ref[:half, :], their_top),
                (mine_ref[half:, :], their_bottom),
            )
        ]
        total = before_ref[...] + (squares[0] + squares[1])
        loss_ref[...] = total
        write_note(send_ref, columns, total)

    shape = (columns, width)
    return pl.pallas_call(
        kernel,
        out_shape=(
            pltpu.VMEM((1, columns), f32), pltpu.VMEM(shape, f32), pltpu.VMEM(shape, f32),
            pltpu.VMEM((columns * (1 + ride) + note_rows, width), bf16),
            *[pltpu.VMEM(shape, bf16)] * (1 - ride),
        ),
        in_specs=vmem(n + 3), out_specs=tuple(vmem(5 - ride)), name="partial_gradient",
        compiler_params=params,
    )(*held(*pieces, mine, theirs, loss))


def join_far(far, got, loss):
    columns, width = far.shape

    def kernel(far_ref, got_ref, loss_ref, send_ref, sum_ref):
        total = far_ref[...] + got_ref[:columns, :].astype(f32)
        send_ref[:columns, :] = total.astype(bf16)
        both = loss_ref[...] + read_note(got_ref, columns, columns)
        sum_ref[...] = both
        write_note(send_ref, columns, both)

    return pl.pallas_call(
        kernel,
        out_shape=(pltpu.VMEM((columns + note_rows, width), bf16), pltpu.VMEM((1, columns), f32)),
        in_specs=vmem(3), out_specs=tuple(vmem(2)), name="join_far", compiler_params=params,
    )(*held(far, got, loss))


def total_loss(loss, got):
    columns = loss.shape[1]

    def kernel(loss_ref, got_ref, out_ref):
        out_ref[...] = loss_ref[...] + read_note(got_ref, columns, columns)

    return pl.pallas_call(
        kernel, out_shape=pltpu.VMEM((1, columns), f32), in_specs=vmem(2), out_specs=vmem(1)[0],
        name="total_loss", compiler_params=params,
    )(*held(loss, got))


def apply_update(half, own, near, far, states, news=()):
    width, columns = own.shape[1], own.shape[0]
    n = len(news)

    def kernel(own_ref, near_ref, far_ref, w_ref, m_ref, v_ref, *refs):
        gradient = own_ref[...] + near_ref[-columns:, :].astype(f32)
        gradient += far_ref[:columns, :].astype(f32)
        where = (slice(None), slice(half * columns, (half + 1) * columns))
        results = adamw(gradient.T, w_ref[where], m_ref[where], v_ref[where])
        for ref, result in zip(refs[n:], results, strict=True):
            ref[...] = result

    shape = jax.ShapeDtypeStruct(states[0].shape, f32)
    block = pl.BlockSpec((width, columns), lambda i: (0, half))
    return pl.pallas_call(
        kernel, grid=(1,), out_shape=(shape,) * 3,
        in_specs=vmem(6) + [pl.BlockSpec(memory_space=pl.ANY)] * n, out_specs=(block,) * 3,
        input_output_aliases={6 + i: i for i in range(n)},
        name="apply_update", compiler_params=params,
    )(*held(own, near, far, *states), *news)


def paired(hidden_states, teacher_weight, student_weight, first_moment, second_moment):
    fsdp = lax.axis_size("fsdp")
    blocks = fsdp // 2
    total_tokens = hidden_states.shape[0] * fsdp * lax.axis_size("tensor")
    columns = student_weight.shape[1] // 2
    halves = [slice(0, columns), slice(columns, 2 * columns)]

    def flip(array, bit):
        return lax.ppermute(array, "fsdp", [(i, i ^ bit) for i in range(fsdp)])

    def swap_cores(array):
        return lax.ppermute(array, "tensor", [(0, 1), (1, 0)])

    def together(*values):
        return lax.optimization_barrier(values)

    column_max = jnp.max(jnp.abs(student_weight), axis=0, keepdims=True)
    keep, send = sort_features(hidden_states, blocks)
    column_max = jnp.maximum(column_max, flip(column_max, 1))
    keep, column_max = together(keep, column_max)
    peer = flip(send, 1)
    near_keep = swap_cores(keep)
    peaks = [column_max] + [flip(column_max, 2 * k) for k in range(1, blocks)]
    column_max = jnp.maximum(jnp.maximum(peaks[0], peaks[1]), jnp.maximum(peaks[2], peaks[3]))
    difference = weight_difference(student_weight, teacher_weight, column_max) * 2.0**15
    coded = difference.astype(jnp.float16)

    far = flip(coded, 4)
    near = flip(coded, 2)
    far, near, near_keep = together(far, near, near_keep)
    across = [flip(far[:, half], 2) for half in halves]
    peer, across[0] = together(peer, across[0])
    pieces = [keep, near_keep, peer, swap_cores(peer)]

    def residual(c):
        parts = [p[:, halves[c]].astype(f32) for p in (difference, near, far)]
        pairs = [high_low(p) for p in (*parts, across[c].astype(f32))]
        return partial_residual(pieces, [p[0] for p in pairs], [p[1] for p in pairs])

    mine, sent = residual(0)
    theirs = flip(sent, 1)
    mine_next, sent_next = residual(1)
    theirs_next = flip(sent_next, 1)

    loss = jnp.zeros((1, columns), f32)
    loss, own, rest, to_across, to_near = partial_gradient(
        pieces, mine, theirs, loss, total_tokens, False
    )
    from_across = flip(to_across, 2)
    theirs_next, from_across = together(theirs_next, from_across)
    loss_next, own_next, rest_next, to_across = partial_gradient(
        pieces, mine_next, theirs_next, loss, total_tokens, True
    )
    from_across_next = flip(to_across, 2)
    from_near = flip(to_near, 2)
    to_far, _ = join_far(rest, from_across, loss)
    to_far, from_near = together(to_far, from_near)
    from_far = flip(to_far, 4)
    states = (student_weight, first_moment, second_moment)
    from_across_next, from_far = together(from_across_next, from_far)
    news = apply_update(0, own, from_near, from_far, states)
    to_far, loss = join_far(rest_next, from_across_next, loss_next)
    from_far_next = flip(to_far, 4)
    from_far_next, *news = together(from_far_next, *news)
    loss = total_loss(loss, from_far_next)
    loss = jnp.sum(loss + swap_cores(loss)).reshape(1) / total_tokens
    news = apply_update(1, own_next, from_across_next, from_far_next, states, news)
    return (*news, loss)


def solution(mesh):
    fsdp, tensor = mesh.shape["fsdp"], mesh.shape["tensor"]

    def per_device(hidden_states, *weights):
        rows = weights[0].shape[0]
        few = fsdp == 8 and tensor == 2 and rows % 128 == 0 and weights[0].shape[1] % 256 == 0
        return (paired if few else generic)(hidden_states, *weights)

    rows = P(("groups", "fsdp"), "tensor")
    in_specs = (P(("groups", "fsdp", "tensor"), None), P("fsdp", "tensor"), rows, rows, rows)
    out_specs = (rows, rows, rows, P("groups"))
    return jax.shard_map(
        per_device, mesh=mesh, in_specs=in_specs, out_specs=out_specs, check_vma=False
    )
```

```python
import math

import jax
import jax.numpy as jnp
from jax import lax
from jax.experimental import pallas as pl
from jax.experimental.pallas import tpu as pltpu
from jax.sharding import PartitionSpec as P

two_pi = 2.0 * math.pi
first_bias = 1.0 - 0.9**20
second_bias = 1.0 - 0.95**20
f32 = jnp.float32
bf16 = jnp.bfloat16


def soft_quantize(weights, quant_scale):
    scaled = weights / quant_scale
    return (quant_scale * (scaled - jnp.sin(two_pi * scaled) / two_pi)).astype(bf16)


def adamw(gradient, student_weight, first_moment, second_moment):
    new_first = 0.9 * first_moment + 0.1 * gradient
    new_second = 0.95 * second_moment + 0.05 * gradient * gradient
    update = new_first / first_bias / (jnp.sqrt(new_second / second_bias) + 1e-08)
    new_student = student_weight - 0.001 * (update + 0.1 * student_weight)
    return new_student, new_first, new_second


def generic(hidden_states, teacher_weight, student_weight, first_moment, second_moment):
    all_inputs = lax.all_gather(hidden_states, "tensor", axis=0, tiled=True)
    total_tokens = all_inputs.shape[0] * lax.axis_size("fsdp")
    local_max = jnp.max(jnp.abs(student_weight), axis=0, keepdims=True)
    quant_scale = (lax.pmax(local_max, "fsdp") + 1e-06) / 7.0
    quantized = soft_quantize(student_weight, quant_scale)
    difference = (quantized.astype(f32) - teacher_weight.astype(f32)).astype(bf16)
    difference = lax.all_gather(difference, "fsdp", axis=0, tiled=True)
    residual = jnp.dot(all_inputs, difference, preferred_element_type=f32)
    squared = jnp.sum(residual * residual).reshape(1)
    distill_loss = lax.psum(squared, ("fsdp", "tensor")) / total_tokens
    grad_out = (residual * (2.0 / total_tokens)).astype(bf16)
    partial = lax.dot_general(
        all_inputs, grad_out, (((0,), (0,)), ((), ())), preferred_element_type=f32
    )
    gradient = lax.psum_scatter(partial, "fsdp", scatter_dimension=0, tiled=True)
    return (*adamw(gradient, student_weight, first_moment, second_moment), distill_loss)


params = pltpu.CompilerParams(vmem_limit_bytes=16 * 2**20)
sine_terms = (
    6.579736267281999,
    -12.987878760960296,
    12.208113946775761,
    -6.6937816308195295,
    2.4016117188086827,
    -0.6033682700805688,
    0.1006404612407522,
)


def vmem(n):
    return [pl.BlockSpec(memory_space=pltpu.VMEM)] * n


def held(*arrays):
    return [pltpu.with_memory_space_constraint(a, pltpu.VMEM) for a in arrays]


def rounded(array):
    return lax.reduce_precision(array, 8, 7)


def high_low(array):
    high = rounded(array)
    return high.astype(bf16), (array - high).astype(bf16)


def weight_difference(student_weight, teacher_weight, column_max):
    quant_scale = (column_max + 1e-06) / 7.0
    scaled = student_weight / quant_scale
    whole = jnp.round(scaled)
    rest = scaled - whole
    square = rest * rest
    series = jnp.full_like(square, sine_terms[-1])
    for term in sine_terms[-2::-1]:
        series = series * square + term
    quantized = rounded(quant_scale * (whole + rest * square * series))
    return quantized - teacher_weight.astype(f32)


early = 3


def sort_features(hidden_states, blocks):
    tokens, features = hidden_states.shape
    width = features // (2 * blocks)

    def kernel(h_ref, keep_ref, most_ref, rest_ref):
        index = lax.axis_index("fsdp")
        rank, half = index // 2, index % 2
        for k in range(blocks):
            block = jnp.bitwise_xor(rank, k) * 2
            where = slice(k * width, (k + 1) * width)
            start = pl.multiple_of((block + half) * width, width)
            keep_ref[:, where] = h_ref[:, pl.ds(start, width)]
            start = pl.multiple_of((block + 1 - half) * width, width)
            if k < early:
                most_ref[:, where] = h_ref[:, pl.ds(start, width)]
            else:
                where = slice((k - early) * width, (k - early + 1) * width)
                rest_ref[:, where] = h_ref[:, pl.ds(start, width)]

    shapes = [pltpu.VMEM((tokens, n * width), bf16) for n in (blocks, early, blocks - early)]
    return pl.pallas_call(
        kernel, out_shape=tuple(shapes), in_specs=vmem(1), out_specs=tuple(vmem(3)),
        name="sort_features", compiler_params=params,
    )(*held(hidden_states))


def locate(pieces, width):
    places, i = [], 0
    for piece in pieces:
        places.append([])
        for array in piece:
            places[-1] += [(i, at) for at in range(0, array.shape[1], width)]
            i += 1
    return places, [array for piece in pieces for array in piece]


def partial_residual(pieces, highs, lows):
    tokens = pieces[0][0].shape[0]
    width, columns = highs[0].shape
    places, flat = locate(pieces, width)
    n, m = len(flat), len(highs)

    def kernel(*refs):
        h_refs, d_refs, (wide_ref, sent_ref) = refs[:n], refs[n : n + 2 * m], refs[n + 2 * m :]
        weights = [
            jnp.concatenate([high[...], low[...]], axis=1)
            for high, low in zip(d_refs[:m], d_refs[m:], strict=True)
        ]
        for i, place in enumerate(places):
            total = jnp.zeros((tokens, 2 * columns), f32)
            for (j, at), weight in zip(place, weights, strict=True):
                total += jnp.dot(
                    h_refs[j][:, at : at + width], weight, preferred_element_type=f32
                )
            total = (total[:, :columns] + total[:, columns:]) * 2.0**-15
            rows = slice(i * tokens, (i + 1) * tokens)
            wide_ref[rows, :] = total
            sent_ref[rows, :] = total.astype(bf16)

    shape = (len(pieces) * tokens, columns)
    return pl.pallas_call(
        kernel,
        out_shape=(pltpu.VMEM(shape, f32), pltpu.VMEM(shape, bf16)),
        in_specs=vmem(n + 2 * m), out_specs=tuple(vmem(2)), name="partial_residual",
        compiler_params=params,
    )(*held(*flat, *highs, *lows))


def split_float(array):
    rows = []
    for _ in range(3):
        rows.append(array.astype(bf16))
        array = array - rows[-1].astype(f32)
    return rows


note_rows = 16


def write_note(ref, start, row):
    width = ref.shape[1]
    parts = [p.astype(f32) for p in split_float(row)]
    parts.append(jnp.zeros((note_rows - 3, row.shape[1]), f32))
    note = jnp.concatenate(parts, axis=0).astype(bf16)
    pad = jnp.zeros((note_rows, width - row.shape[1]), bf16)
    ref[start : start + note_rows, :] = jnp.concatenate([note, pad], axis=1)


def read_note(ref, start, columns):
    note = ref[start : start + note_rows, :columns].astype(f32)
    return note[0:1, :] + note[1:2, :] + note[2:3, :]


def partial_gradient(pieces, mine, theirs, loss, total_tokens, ride):
    tokens, features = pieces[0][0].shape
    width, columns = features // 4, mine.shape[1]
    places, flat = locate(pieces, width)
    n = len(flat)

    def kernel(*refs):
        h_refs, mine_ref, theirs_ref, before_ref = refs[:n], *refs[n : n + 3]
        loss_ref, own_ref, far_ref, send_ref, *near_refs = refs[n + 3 :]
        half = len(places) * tokens // 2
        top, bottom = mine_ref[:half, :], mine_ref[half:, :]
        their_bottom = theirs_ref[:half, :].astype(f32)
        their_top = theirs_ref[half:, :].astype(f32)
        top, bottom = top + their_top, bottom + their_bottom
        grad_out = jnp.concatenate([top, bottom], axis=0) * (2.0 / total_tokens)
        grad_out = grad_out.astype(bf16)
        for k in (3, 1, 2, 0):
            total = jnp.zeros((columns, width), f32)
            for i, place in enumerate(places):
                j, at = place[k]
                total += lax.dot_general(
                    grad_out[i * tokens : (i + 1) * tokens, :],
                    h_refs[j][:, at : at + width],
                    (((0,), (0,)), ((), ())), preferred_element_type=f32,
                )
            if k == 3:
                send_ref[:columns, :] = total.astype(bf16)
            elif k == 1:
                near = total.astype(bf16)
                if ride:
                    send_ref[columns + note_rows :, :] = near
                else:
                    near_refs[0][...] = near
            elif k == 2:
                far_ref[...] = total
            else:
                own_ref[...] = total
        squares = [
            jnp.sum(jnp.square(a.astype(bf16).astype(f32) + b), axis=0, keepdims=True)
            for a, b in (
                (mine_ref[:half, :], their_top),
                (mine_ref[half:, :], their_bottom),
            )
        ]
        total = before_ref[...] + (squares[0] + squares[1])
        loss_ref[...] = total
        write_note(send_ref, columns, total)

    shape = (columns, width)
    return pl.pallas_call(
        kernel,
        out_shape=(
            pltpu.VMEM((1, columns), f32), pltpu.VMEM(shape, f32), pltpu.VMEM(shape, f32),
            pltpu.VMEM((columns * (1 + ride) + note_rows, width), bf16),
            *[pltpu.VMEM(shape, bf16)] * (1 - ride),
        ),
        in_specs=vmem(n + 3), out_specs=tuple(vmem(5 - ride)), name="partial_gradient",
        compiler_params=params,
    )(*held(*flat, mine, theirs, loss))


def join_far(far, got, loss):
    columns, width = far.shape

    def kernel(far_ref, got_ref, loss_ref, send_ref, sum_ref):
        total = far_ref[...] + got_ref[:columns, :].astype(f32)
        send_ref[:columns, :] = total.astype(bf16)
        both = loss_ref[...] + read_note(got_ref, columns, columns)
        sum_ref[...] = both
        write_note(send_ref, columns, both)

    return pl.pallas_call(
        kernel,
        out_shape=(pltpu.VMEM((columns + note_rows, width), bf16), pltpu.VMEM((1, columns), f32)),
        in_specs=vmem(3), out_specs=tuple(vmem(2)), name="join_far", compiler_params=params,
    )(*held(far, got, loss))


def total_loss(loss, got):
    columns = loss.shape[1]

    def kernel(loss_ref, got_ref, out_ref):
        out_ref[...] = loss_ref[...] + read_note(got_ref, columns, columns)

    return pl.pallas_call(
        kernel, out_shape=pltpu.VMEM((1, columns), f32), in_specs=vmem(2), out_specs=vmem(1)[0],
        name="total_loss", compiler_params=params,
    )(*held(loss, got))


def apply_update(half, own, near, far, states, news=()):
    width, columns = own.shape[1], own.shape[0]
    n = len(news)

    def kernel(own_ref, near_ref, far_ref, w_ref, m_ref, v_ref, *refs):
        gradient = own_ref[...] + near_ref[-columns:, :].astype(f32)
        gradient += far_ref[:columns, :].astype(f32)
        where = (slice(None), slice(half * columns, (half + 1) * columns))
        results = adamw(gradient.T, w_ref[where], m_ref[where], v_ref[where])
        for ref, result in zip(refs[n:], results, strict=True):
            ref[...] = result

    shape = jax.ShapeDtypeStruct(states[0].shape, f32)
    block = pl.BlockSpec((width, columns), lambda i: (0, half))
    return pl.pallas_call(
        kernel, grid=(1,), out_shape=(shape,) * 3,
        in_specs=vmem(6) + [pl.BlockSpec(memory_space=pl.ANY)] * n, out_specs=(block,) * 3,
        input_output_aliases={6 + i: i for i in range(n)},
        name="apply_update", compiler_params=params,
    )(*held(own, near, far, *states), *news)


def paired(hidden_states, teacher_weight, student_weight, first_moment, second_moment):
    fsdp = lax.axis_size("fsdp")
    blocks = fsdp // 2
    total_tokens = hidden_states.shape[0] * fsdp * lax.axis_size("tensor")
    columns = student_weight.shape[1] // 2
    halves = [slice(0, columns), slice(columns, 2 * columns)]

    def flip(array, bit):
        return lax.ppermute(array, "fsdp", [(i, i ^ bit) for i in range(fsdp)])

    def swap_cores(array):
        return lax.ppermute(array, "tensor", [(0, 1), (1, 0)])

    def together(*values):
        return lax.optimization_barrier(values)

    column_max = jnp.max(jnp.abs(student_weight), axis=0, keepdims=True)
    keep, *sends = sort_features(hidden_states, blocks)
    column_max = jnp.maximum(column_max, flip(column_max, 1))
    keep, column_max = together(keep, column_max)
    peers = [flip(send, 1) for send in sends]
    near_keep = swap_cores(keep)
    column_max = jnp.maximum(column_max, flip(column_max, 2))
    column_max = jnp.maximum(column_max, flip(column_max, 4))
    difference = weight_difference(student_weight, teacher_weight, column_max) * 2.0**15
    coded = difference.astype(jnp.float16)

    far = flip(coded, 4)
    near = flip(coded, 2)
    far, near, peers[0], near_keep = together(far, near, peers[0], near_keep)
    across = [flip(far[:, half], 2) for half in halves]
    peers[1], across[0] = together(peers[1], across[0])
    pieces = [(keep,), (near_keep,), peers, [swap_cores(peer) for peer in peers]]

    def residual(c):
        parts = [p[:, halves[c]].astype(f32) for p in (difference, near, far)]
        pairs = [high_low(p) for p in (*parts, across[c].astype(f32))]
        return partial_residual(pieces, [p[0] for p in pairs], [p[1] for p in pairs])

    mine, sent = residual(0)
    theirs = flip(sent, 1)
    mine_next, sent_next = residual(1)
    theirs_next = flip(sent_next, 1)

    loss = jnp.zeros((1, columns), f32)
    loss, own, rest, to_across, to_near = partial_gradient(
        pieces, mine, theirs, loss, total_tokens, False
    )
    from_across = flip(to_across, 2)
    theirs_next, from_across = together(theirs_next, from_across)
    loss_next, own_next, rest_next, to_across, to_near_next = partial_gradient(
        pieces, mine_next, theirs_next, loss, total_tokens, False
    )
    from_near = flip(to_near, 2)
    from_across, from_near, to_across = together(from_across, from_near, to_across)
    from_across_next = flip(to_across, 2)
    to_far, _ = join_far(rest, from_across, loss)
    from_far = flip(to_far, 4)
    states = (student_weight, first_moment, second_moment)
    news = apply_update(0, own, from_near, from_far, states)
    to_far, loss = join_far(rest_next, from_across_next, loss_next)
    from_far_next = flip(to_far, 4)
    from_near_next = flip(to_near_next, 2)
    from_far_next, *news = together(from_far_next, *news)
    loss = total_loss(loss, from_far_next)
    loss = jnp.sum(loss + swap_cores(loss)).reshape(1) / total_tokens
    news = apply_update(1, own_next, from_near_next, from_far_next, states, news)
    return (*news, loss)


def solution(mesh):
    fsdp, tensor = mesh.shape["fsdp"], mesh.shape["tensor"]

    def per_device(hidden_states, *weights):
        rows = weights[0].shape[0]
        few = fsdp == 8 and tensor == 2 and rows % 128 == 0 and weights[0].shape[1] % 256 == 0
        return (paired if few else generic)(hidden_states, *weights)

    rows = P(("groups", "fsdp"), "tensor")
    in_specs = (P(("groups", "fsdp", "tensor"), None), P("fsdp", "tensor"), rows, rows, rows)
    out_specs = (rows, rows, rows, P("groups"))
    return jax.shard_map(
        per_device, mesh=mesh, in_specs=in_specs, out_specs=out_specs, check_vma=False
    )
```

```python
import math

import jax
import jax.numpy as jnp
from jax import lax
from jax.experimental import pallas as pl
from jax.experimental.pallas import tpu as pltpu
from jax.sharding import PartitionSpec as P

two_pi = 2.0 * math.pi
first_bias = 1.0 - 0.9**20
second_bias = 1.0 - 0.95**20
f32 = jnp.float32
bf16 = jnp.bfloat16


def soft_quantize(weights, quant_scale):
    scaled = weights / quant_scale
    return (quant_scale * (scaled - jnp.sin(two_pi * scaled) / two_pi)).astype(bf16)


def adamw(gradient, student_weight, first_moment, second_moment):
    new_first = 0.9 * first_moment + 0.1 * gradient
    new_second = 0.95 * second_moment + 0.05 * gradient * gradient
    update = new_first / first_bias / (jnp.sqrt(new_second / second_bias) + 1e-08)
    new_student = student_weight - 0.001 * (update + 0.1 * student_weight)
    return new_student, new_first, new_second


def generic(hidden_states, teacher_weight, student_weight, first_moment, second_moment):
    all_inputs = lax.all_gather(hidden_states, "tensor", axis=0, tiled=True)
    total_tokens = all_inputs.shape[0] * lax.axis_size("fsdp")
    local_max = jnp.max(jnp.abs(student_weight), axis=0, keepdims=True)
    quant_scale = (lax.pmax(local_max, "fsdp") + 1e-06) / 7.0
    quantized = soft_quantize(student_weight, quant_scale)
    difference = (quantized.astype(f32) - teacher_weight.astype(f32)).astype(bf16)
    difference = lax.all_gather(difference, "fsdp", axis=0, tiled=True)
    residual = jnp.dot(all_inputs, difference, preferred_element_type=f32)
    squared = jnp.sum(residual * residual).reshape(1)
    distill_loss = lax.psum(squared, ("fsdp", "tensor")) / total_tokens
    grad_out = (residual * (2.0 / total_tokens)).astype(bf16)
    partial = lax.dot_general(
        all_inputs, grad_out, (((0,), (0,)), ((), ())), preferred_element_type=f32
    )
    gradient = lax.psum_scatter(partial, "fsdp", scatter_dimension=0, tiled=True)
    return (*adamw(gradient, student_weight, first_moment, second_moment), distill_loss)


params = pltpu.CompilerParams(vmem_limit_bytes=16 * 2**20)
sine_terms = (
    6.579736267281999,
    -12.987878760960296,
    12.208113946775761,
    -6.6937816308195295,
    2.4016117188086827,
    -0.6033682700805688,
    0.1006404612407522,
)


def vmem(n):
    return [pl.BlockSpec(memory_space=pltpu.VMEM)] * n


def held(*arrays):
    return [pltpu.with_memory_space_constraint(a, pltpu.VMEM) for a in arrays]


def rounded(array):
    return lax.reduce_precision(array, 8, 7)


def high_low(array):
    high = rounded(array)
    return high.astype(bf16), (array - high).astype(bf16)


def weight_difference(student_weight, teacher_weight, column_max):
    quant_scale = (column_max + 1e-06) / 7.0
    scaled = student_weight / quant_scale
    whole = jnp.round(scaled)
    rest = scaled - whole
    square = rest * rest
    series = jnp.full_like(square, sine_terms[-1])
    for term in sine_terms[-2::-1]:
        series = series * square + term
    quantized = rounded(quant_scale * (whole + rest * square * series))
    return quantized - teacher_weight.astype(f32)


early = 3


def sort_features(hidden_states, blocks):
    tokens, features = hidden_states.shape
    width = features // (2 * blocks)

    def kernel(h_ref, keep_ref, most_ref, rest_ref):
        index = lax.axis_index("fsdp")
        rank, half = index // 2, index % 2
        for k in range(blocks):
            block = jnp.bitwise_xor(rank, k) * 2
            where = slice(k * width, (k + 1) * width)
            start = pl.multiple_of((block + half) * width, width)
            keep_ref[:, where] = h_ref[:, pl.ds(start, width)]
            start = pl.multiple_of((block + 1 - half) * width, width)
            if k < early:
                most_ref[:, where] = h_ref[:, pl.ds(start, width)]
            else:
                where = slice((k - early) * width, (k - early + 1) * width)
                rest_ref[:, where] = h_ref[:, pl.ds(start, width)]

    shapes = [pltpu.VMEM((tokens, n * width), bf16) for n in (blocks, early, blocks - early)]
    return pl.pallas_call(
        kernel, out_shape=tuple(shapes), in_specs=vmem(1), out_specs=tuple(vmem(3)),
        name="sort_features", compiler_params=params,
    )(*held(hidden_states))


def locate(pieces, width):
    places, i = [], 0
    for piece in pieces:
        places.append([])
        for array in piece:
            places[-1] += [(i, at) for at in range(0, array.shape[1], width)]
            i += 1
    return places, [array for piece in pieces for array in piece]


def partial_residual(pieces, highs, lows):
    tokens = pieces[0][0].shape[0]
    width, columns = highs[0].shape
    places, flat = locate(pieces, width)
    n, m = len(flat), len(highs)

    def kernel(*refs):
        h_refs, d_refs, (wide_ref, sent_ref) = refs[:n], refs[n : n + 2 * m], refs[n + 2 * m :]
        weights = [
            jnp.concatenate([high[...], low[...]], axis=1)
            for high, low in zip(d_refs[:m], d_refs[m:], strict=True)
        ]
        for i, place in enumerate(places):
            total = jnp.zeros((tokens, 2 * columns), f32)
            for (j, at), weight in zip(place, weights, strict=True):
                total += jnp.dot(
                    h_refs[j][:, at : at + width], weight, preferred_element_type=f32
                )
            total = (total[:, :columns] + total[:, columns:]) * 2.0**-15
            rows = slice(i * tokens, (i + 1) * tokens)
            wide_ref[rows, :] = total
            sent_ref[rows, :] = total.astype(bf16)

    shape = (len(pieces) * tokens, columns)
    return pl.pallas_call(
        kernel,
        out_shape=(pltpu.VMEM(shape, f32), pltpu.VMEM(shape, bf16)),
        in_specs=vmem(n + 2 * m), out_specs=tuple(vmem(2)), name="partial_residual",
        compiler_params=params,
    )(*held(*flat, *highs, *lows))


def split_float(array):
    rows = []
    for _ in range(3):
        rows.append(array.astype(bf16))
        array = array - rows[-1].astype(f32)
    return rows


note_rows = 8


def write_note(ref, start, row):
    width = ref.shape[1]
    parts = [p.astype(f32) for p in split_float(row)]
    parts.append(jnp.zeros((note_rows - 3, row.shape[1]), f32))
    note = jnp.concatenate(parts, axis=0).astype(bf16)
    pad = jnp.zeros((note_rows, width - row.shape[1]), bf16)
    ref[start : start + note_rows, :] = jnp.concatenate([note, pad], axis=1)


def read_note(ref, start, columns):
    note = ref[start : start + note_rows, :columns].astype(f32)
    return note[0:1, :] + note[1:2, :] + note[2:3, :]


def partial_gradient(pieces, mine, theirs, loss, total_tokens, noted):
    tokens, features = pieces[0][0].shape
    width, columns = features // 4, mine.shape[1]
    places, flat = locate(pieces, width)
    n = len(flat)

    def kernel(*refs):
        h_refs, mine_ref, theirs_ref, before_ref = refs[:n], *refs[n : n + 3]
        loss_ref, own_ref, far_ref, send_ref, near_ref = refs[n + 3 :]
        half = len(places) * tokens // 2
        top, bottom = mine_ref[:half, :], mine_ref[half:, :]
        their_bottom = theirs_ref[:half, :].astype(f32)
        their_top = theirs_ref[half:, :].astype(f32)
        top, bottom = top + their_top, bottom + their_bottom
        grad_out = jnp.concatenate([top, bottom], axis=0) * (2.0 / total_tokens)
        grad_out = grad_out.astype(bf16)
        for k in (3, 1, 2, 0):
            total = jnp.zeros((columns, width), f32)
            for i, place in enumerate(places):
                j, at = place[k]
                total += lax.dot_general(
                    grad_out[i * tokens : (i + 1) * tokens, :],
                    h_refs[j][:, at : at + width],
                    (((0,), (0,)), ((), ())), preferred_element_type=f32,
                )
            if k == 3:
                send_ref[:columns, :] = total.astype(bf16)
            elif k == 1:
                near_ref[...] = total.astype(bf16)
            elif k == 2:
                far_ref[...] = total
            else:
                own_ref[...] = total
        squares = [
            jnp.sum(jnp.square(a.astype(bf16).astype(f32) + b), axis=0, keepdims=True)
            for a, b in (
                (mine_ref[:half, :], their_top),
                (mine_ref[half:, :], their_bottom),
            )
        ]
        total = before_ref[...] + (squares[0] + squares[1])
        loss_ref[...] = total
        if noted:
            write_note(send_ref, columns, total)

    shape = (columns, width)
    return pl.pallas_call(
        kernel,
        out_shape=(
            pltpu.VMEM((1, columns), f32), pltpu.VMEM(shape, f32), pltpu.VMEM(shape, f32),
            pltpu.VMEM((columns + note_rows * noted, width), bf16), pltpu.VMEM(shape, bf16),
        ),
        in_specs=vmem(n + 3), out_specs=tuple(vmem(5)), name="partial_gradient",
        compiler_params=params,
    )(*held(*flat, mine, theirs, loss))


def join_far(far, got, loss):
    columns, width = far.shape

    def kernel(far_ref, got_ref, loss_ref, send_ref, sum_ref):
        total = far_ref[...] + got_ref[:columns, :].astype(f32)
        send_ref[:columns, :] = total.astype(bf16)
        both = loss_ref[...]
        if got_ref.shape[0] > columns:
            both += read_note(got_ref, columns, columns)
        sum_ref[...] = both
        write_note(send_ref, columns, both)

    return pl.pallas_call(
        kernel,
        out_shape=(pltpu.VMEM((columns + note_rows, width), bf16), pltpu.VMEM((1, columns), f32)),
        in_specs=vmem(3), out_specs=tuple(vmem(2)), name="join_far", compiler_params=params,
    )(*held(far, got, loss))


def total_loss(loss, got):
    columns = loss.shape[1]

    def kernel(loss_ref, got_ref, out_ref):
        out_ref[...] = loss_ref[...] + read_note(got_ref, columns, columns)

    return pl.pallas_call(
        kernel, out_shape=pltpu.VMEM((1, columns), f32), in_specs=vmem(2), out_specs=vmem(1)[0],
        name="total_loss", compiler_params=params,
    )(*held(loss, got))


def apply_update(half, own, near, far, states, news=()):
    width, columns = own.shape[1], own.shape[0]
    n = len(news)

    def kernel(own_ref, near_ref, far_ref, w_ref, m_ref, v_ref, *refs):
        gradient = own_ref[...] + near_ref[-columns:, :].astype(f32)
        gradient += far_ref[:columns, :].astype(f32)
        where = (slice(None), slice(half * columns, (half + 1) * columns))
        results = adamw(gradient.T, w_ref[where], m_ref[where], v_ref[where])
        for ref, result in zip(refs[n:], results, strict=True):
            ref[...] = result

    shape = jax.ShapeDtypeStruct(states[0].shape, f32)
    block = pl.BlockSpec((width, columns), lambda i: (0, half))
    return pl.pallas_call(
        kernel, grid=(1,), out_shape=(shape,) * 3,
        in_specs=vmem(6) + [pl.BlockSpec(memory_space=pl.ANY)] * n, out_specs=(block,) * 3,
        input_output_aliases={6 + i: i for i in range(n)},
        name="apply_update", compiler_params=params,
    )(*held(own, near, far, *states), *news)


def paired(hidden_states, teacher_weight, student_weight, first_moment, second_moment):
    fsdp = lax.axis_size("fsdp")
    blocks = fsdp // 2
    total_tokens = hidden_states.shape[0] * fsdp * lax.axis_size("tensor")
    columns = student_weight.shape[1] // 2
    halves = [slice(0, columns), slice(columns, 2 * columns)]

    def flip(array, bit):
        return lax.ppermute(array, "fsdp", [(i, i ^ bit) for i in range(fsdp)])

    def swap_cores(array):
        return lax.ppermute(array, "tensor", [(0, 1), (1, 0)])

    def together(*values):
        return lax.optimization_barrier(values)

    column_max = jnp.max(jnp.abs(student_weight), axis=0, keepdims=True)
    keep, *sends = sort_features(hidden_states, blocks)
    column_max = jnp.maximum(column_max, flip(column_max, 1))
    keep, column_max = together(keep, column_max)
    peers = [flip(send, 1) for send in sends]
    near_keep = swap_cores(keep)
    column_max = jnp.maximum(column_max, flip(column_max, 2))
    column_max = jnp.maximum(column_max, flip(column_max, 4))
    difference = weight_difference(student_weight, teacher_weight, column_max) * 2.0**15
    coded = difference.astype(jnp.float16)

    far = flip(coded, 4)
    near = flip(coded, 2)
    far, near, peers[0], near_keep = together(far, near, peers[0], near_keep)
    across = [flip(far[:, half], 2) for half in halves]
    peers[1], across[0] = together(peers[1], across[0])
    pieces = [(keep,), (near_keep,), peers, [swap_cores(peer) for peer in peers]]

    def residual(c):
        parts = [p[:, halves[c]].astype(f32) for p in (difference, near, far)]
        pairs = [high_low(p) for p in (*parts, across[c].astype(f32))]
        return partial_residual(pieces, [p[0] for p in pairs], [p[1] for p in pairs])

    mine, sent = residual(0)
    theirs = flip(sent, 1)
    mine_next, sent_next = residual(1)
    theirs_next = flip(sent_next, 1)

    loss = jnp.zeros((1, columns), f32)
    loss, own, rest, to_across, to_near = partial_gradient(
        pieces, mine, theirs, loss, total_tokens, False
    )
    from_across = flip(to_across, 2)
    theirs_next, from_across = together(theirs_next, from_across)
    loss_next, own_next, rest_next, to_across, to_near_next = partial_gradient(
        pieces, mine_next, theirs_next, loss, total_tokens, True
    )
    from_near = flip(to_near, 2)
    from_across, from_near, to_across = together(from_across, from_near, to_across)
    from_across_next = flip(to_across, 2)
    to_far, _ = join_far(rest, from_across, loss)
    from_far = flip(to_far, 4)
    states = (student_weight, first_moment, second_moment)
    news = apply_update(0, own, from_near, from_far, states)
    to_far, loss = join_far(rest_next, from_across_next, loss_next)
    from_far_next = flip(to_far, 4)
    from_near_next = flip(to_near_next, 2)
    from_far_next, *news = together(from_far_next, *news)
    loss = total_loss(loss, from_far_next)
    loss = jnp.sum(loss + swap_cores(loss)).reshape(1) / total_tokens
    news = apply_update(1, own_next, from_near_next, from_far_next, states, news)
    return (*news, loss)


def solution(mesh):
    fsdp, tensor = mesh.shape["fsdp"], mesh.shape["tensor"]

    def per_device(hidden_states, *weights):
        rows = weights[0].shape[0]
        few = fsdp == 8 and tensor == 2 and rows % 128 == 0 and weights[0].shape[1] % 256 == 0
        return (paired if few else generic)(hidden_states, *weights)

    rows = P(("groups", "fsdp"), "tensor")
    in_specs = (P(("groups", "fsdp", "tensor"), None), P("fsdp", "tensor"), rows, rows, rows)
    out_specs = (rows, rows, rows, P("groups"))
    return jax.shard_map(
        per_device, mesh=mesh, in_specs=in_specs, out_specs=out_specs, check_vma=False
    )
```

```python
import math

import jax
import jax.numpy as jnp
from jax import lax
from jax.experimental import pallas as pl
from jax.experimental.pallas import tpu as pltpu
from jax.sharding import PartitionSpec as P

two_pi = 2.0 * math.pi
first_bias = 1.0 - 0.9**20
second_bias = 1.0 - 0.95**20
f32 = jnp.float32
bf16 = jnp.bfloat16


def soft_quantize(weights, quant_scale):
    scaled = weights / quant_scale
    return (quant_scale * (scaled - jnp.sin(two_pi * scaled) / two_pi)).astype(bf16)


def adamw(gradient, student_weight, first_moment, second_moment):
    new_first = 0.9 * first_moment + 0.1 * gradient
    new_second = 0.95 * second_moment + 0.05 * gradient * gradient
    update = new_first / first_bias / (jnp.sqrt(new_second / second_bias) + 1e-08)
    new_student = student_weight - 0.001 * (update + 0.1 * student_weight)
    return new_student, new_first, new_second


def generic(hidden_states, teacher_weight, student_weight, first_moment, second_moment):
    all_inputs = lax.all_gather(hidden_states, "tensor", axis=0, tiled=True)
    total_tokens = all_inputs.shape[0] * lax.axis_size("fsdp")
    local_max = jnp.max(jnp.abs(student_weight), axis=0, keepdims=True)
    quant_scale = (lax.pmax(local_max, "fsdp") + 1e-06) / 7.0
    quantized = soft_quantize(student_weight, quant_scale)
    difference = (quantized.astype(f32) - teacher_weight.astype(f32)).astype(bf16)
    difference = lax.all_gather(difference, "fsdp", axis=0, tiled=True)
    residual = jnp.dot(all_inputs, difference, preferred_element_type=f32)
    squared = jnp.sum(residual * residual).reshape(1)
    distill_loss = lax.psum(squared, ("fsdp", "tensor")) / total_tokens
    grad_out = (residual * (2.0 / total_tokens)).astype(bf16)
    partial = lax.dot_general(
        all_inputs, grad_out, (((0,), (0,)), ((), ())), preferred_element_type=f32
    )
    gradient = lax.psum_scatter(partial, "fsdp", scatter_dimension=0, tiled=True)
    return (*adamw(gradient, student_weight, first_moment, second_moment), distill_loss)


params = pltpu.CompilerParams(vmem_limit_bytes=16 * 2**20)
sine_terms = (
    6.579736267281999,
    -12.987878760960296,
    12.208113946775761,
    -6.6937816308195295,
    2.4016117188086827,
    -0.6033682700805688,
    0.1006404612407522,
)


def vmem(n):
    return [pl.BlockSpec(memory_space=pltpu.VMEM)] * n


def held(*arrays):
    return [pltpu.with_memory_space_constraint(a, pltpu.VMEM) for a in arrays]


def rounded(array):
    return lax.reduce_precision(array, 8, 7)


def high_low(array):
    high = rounded(array)
    return high.astype(bf16), (array - high).astype(bf16)


def weight_difference(student_weight, teacher_weight, column_max):
    quant_scale = (column_max + 1e-06) / 7.0
    scaled = student_weight / quant_scale
    whole = jnp.round(scaled)
    rest = scaled - whole
    square = rest * rest
    series = jnp.full_like(square, sine_terms[-1])
    for term in sine_terms[-2::-1]:
        series = series * square + term
    quantized = rounded(quant_scale * (whole + rest * square * series))
    return quantized - teacher_weight.astype(f32)


early = 3


def sort_features(hidden_states, blocks):
    tokens, features = hidden_states.shape
    width = features // (2 * blocks)

    def kernel(h_ref, keep_ref, most_ref, rest_ref):
        index = lax.axis_index("fsdp")
        rank, half = index // 2, index % 2
        for k in range(blocks):
            block = jnp.bitwise_xor(rank, k) * 2
            where = slice(k * width, (k + 1) * width)
            start = pl.multiple_of((block + half) * width, width)
            keep_ref[:, where] = h_ref[:, pl.ds(start, width)]
            start = pl.multiple_of((block + 1 - half) * width, width)
            if k < early:
                most_ref[:, where] = h_ref[:, pl.ds(start, width)]
            else:
                where = slice((k - early) * width, (k - early + 1) * width)
                rest_ref[:, where] = h_ref[:, pl.ds(start, width)]

    shapes = [pltpu.VMEM((tokens, n * width), bf16) for n in (blocks, early, blocks - early)]
    return pl.pallas_call(
        kernel, out_shape=tuple(shapes), in_specs=vmem(1), out_specs=tuple(vmem(3)),
        name="sort_features", compiler_params=params,
    )(*held(hidden_states))


def locate(pieces, width):
    places, i = [], 0
    for piece in pieces:
        places.append([])
        for array in piece:
            places[-1] += [(i, at) for at in range(0, array.shape[1], width)]
            i += 1
    return places, [array for piece in pieces for array in piece]


def partial_residual(pieces, highs, lows):
    tokens = pieces[0][0].shape[0]
    width, columns = highs[0].shape
    places, flat = locate(pieces, width)
    n, m = len(flat), len(highs)

    def kernel(*refs):
        h_refs, d_refs, (wide_ref, sent_ref) = refs[:n], refs[n : n + 2 * m], refs[n + 2 * m :]
        weights = [
            jnp.concatenate([high[...], low[...]], axis=1)
            for high, low in zip(d_refs[:m], d_refs[m:], strict=True)
        ]
        for i, place in enumerate(places):
            total = jnp.zeros((tokens, 2 * columns), f32)
            for (j, at), weight in zip(place, weights, strict=True):
                total += jnp.dot(
                    h_refs[j][:, at : at + width], weight, preferred_element_type=f32
                )
            total = (total[:, :columns] + total[:, columns:]) * 2.0**-15
            rows = slice(i * tokens, (i + 1) * tokens)
            wide_ref[rows, :] = total
            sent_ref[rows, :] = total.astype(bf16)

    shape = (len(pieces) * tokens, columns)
    return pl.pallas_call(
        kernel,
        out_shape=(pltpu.VMEM(shape, f32), pltpu.VMEM(shape, bf16)),
        in_specs=vmem(n + 2 * m), out_specs=tuple(vmem(2)), name="partial_residual",
        compiler_params=params,
    )(*held(*flat, *highs, *lows))


def split_float(array):
    rows = []
    for _ in range(3):
        rows.append(array.astype(bf16))
        array = array - rows[-1].astype(f32)
    return rows


note_rows = 8


def write_note(ref, start, row):
    width = ref.shape[1]
    parts = [p.astype(f32) for p in split_float(row)]
    parts.append(jnp.zeros((note_rows - 3, row.shape[1]), f32))
    note = jnp.concatenate(parts, axis=0).astype(bf16)
    pad = jnp.zeros((note_rows, width - row.shape[1]), bf16)
    ref[start : start + note_rows, :] = jnp.concatenate([note, pad], axis=1)


def read_note(ref, start, columns):
    note = ref[start : start + note_rows, :columns].astype(f32)
    return note[0:1, :] + note[1:2, :] + note[2:3, :]


def partial_gradient(pieces, mine, theirs, loss, total_tokens, noted):
    tokens, features = pieces[0][0].shape
    width, columns = features // 4, mine.shape[1]
    places, flat = locate(pieces, width)
    n = len(flat)

    def kernel(*refs):
        h_refs, mine_ref, theirs_ref, before_ref = refs[:n], *refs[n : n + 3]
        loss_ref, own_ref, far_ref, send_ref, near_ref = refs[n + 3 :]
        half = len(places) * tokens // 2
        top, bottom = mine_ref[:half, :], mine_ref[half:, :]
        their_bottom = theirs_ref[:half, :].astype(f32)
        their_top = theirs_ref[half:, :].astype(f32)
        top, bottom = top + their_top, bottom + their_bottom
        grad_out = jnp.concatenate([top, bottom], axis=0) * (2.0 / total_tokens)
        grad_out = grad_out.astype(bf16)
        for k in (3, 1, 2, 0):
            total = jnp.zeros((columns, width), f32)
            for i, place in enumerate(places):
                j, at = place[k]
                total += lax.dot_general(
                    grad_out[i * tokens : (i + 1) * tokens, :],
                    h_refs[j][:, at : at + width],
                    (((0,), (0,)), ((), ())), preferred_element_type=f32,
                )
            if k == 3:
                send_ref[:columns, :] = total.astype(bf16)
            elif k == 1:
                near_ref[...] = total.astype(bf16)
            elif k == 2:
                far_ref[...] = total
            else:
                own_ref[...] = total
        squares = [
            jnp.sum(jnp.square(a.astype(bf16).astype(f32) + b), axis=0, keepdims=True)
            for a, b in (
                (mine_ref[:half, :], their_top),
                (mine_ref[half:, :], their_bottom),
            )
        ]
        total = before_ref[...] + (squares[0] + squares[1])
        loss_ref[...] = total
        if noted:
            write_note(send_ref, columns, total)

    shape = (columns, width)
    return pl.pallas_call(
        kernel,
        out_shape=(
            pltpu.VMEM((1, columns), f32), pltpu.VMEM(shape, f32), pltpu.VMEM(shape, f32),
            pltpu.VMEM((columns + note_rows * noted, width), bf16), pltpu.VMEM(shape, bf16),
        ),
        in_specs=vmem(n + 3), out_specs=tuple(vmem(5)), name="partial_gradient",
        compiler_params=params,
    )(*held(*flat, mine, theirs, loss))


def join_far(far, got, loss):
    columns, width = far.shape

    def kernel(far_ref, got_ref, loss_ref, send_ref, sum_ref):
        total = far_ref[...] + got_ref[:columns, :].astype(f32)
        send_ref[:columns, :] = total.astype(bf16)
        both = loss_ref[...]
        if got_ref.shape[0] > columns:
            both += read_note(got_ref, columns, columns)
        sum_ref[...] = both
        write_note(send_ref, columns, both)

    return pl.pallas_call(
        kernel,
        out_shape=(pltpu.VMEM((columns + note_rows, width), bf16), pltpu.VMEM((1, columns), f32)),
        in_specs=vmem(3), out_specs=tuple(vmem(2)), name="join_far", compiler_params=params,
    )(*held(far, got, loss))


def total_loss(loss, got, total_tokens):
    columns = loss.shape[1]

    def kernel(loss_ref, got_ref, out_ref):
        out_ref[...] = (loss_ref[...] + read_note(got_ref, columns, columns)) / total_tokens

    return pl.pallas_call(
        kernel, out_shape=pltpu.VMEM((1, columns), f32), in_specs=vmem(2), out_specs=vmem(1)[0],
        name="total_loss", compiler_params=params,
    )(*held(loss, got))


def apply_update(half, own, near, far, states, news=()):
    width, columns = own.shape[1], own.shape[0]
    n = len(news)

    def kernel(own_ref, near_ref, far_ref, w_ref, m_ref, v_ref, *refs):
        gradient = own_ref[...] + near_ref[-columns:, :].astype(f32)
        gradient += far_ref[:columns, :].astype(f32)
        where = (slice(None), slice(half * columns, (half + 1) * columns))
        results = adamw(gradient.T, w_ref[where], m_ref[where], v_ref[where])
        for ref, result in zip(refs[n:], results, strict=True):
            ref[...] = result

    shape = jax.ShapeDtypeStruct(states[0].shape, f32)
    block = pl.BlockSpec((width, columns), lambda i: (0, half))
    return pl.pallas_call(
        kernel, grid=(1,), out_shape=(shape,) * 3,
        in_specs=vmem(6) + [pl.BlockSpec(memory_space=pl.ANY)] * n, out_specs=(block,) * 3,
        input_output_aliases={6 + i: i for i in range(n)},
        name="apply_update", compiler_params=params,
    )(*held(own, near, far, *states), *news)


def paired(hidden_states, teacher_weight, student_weight, first_moment, second_moment):
    fsdp = lax.axis_size("fsdp")
    blocks = fsdp // 2
    total_tokens = hidden_states.shape[0] * fsdp * lax.axis_size("tensor")
    columns = student_weight.shape[1] // 2
    halves = [slice(0, columns), slice(columns, 2 * columns)]

    def flip(array, bit):
        return lax.ppermute(array, "fsdp", [(i, i ^ bit) for i in range(fsdp)])

    def swap_cores(array):
        return lax.ppermute(array, "tensor", [(0, 1), (1, 0)])

    def together(*values):
        return lax.optimization_barrier(values)

    column_max = jnp.max(jnp.abs(student_weight), axis=0, keepdims=True)
    keep, *sends = sort_features(hidden_states, blocks)
    column_max = jnp.maximum(column_max, flip(column_max, 1))
    keep, column_max = together(keep, column_max)
    peers = [flip(send, 1) for send in sends]
    near_keep = swap_cores(keep)
    column_max = jnp.maximum(column_max, flip(column_max, 2))
    column_max = jnp.maximum(column_max, flip(column_max, 4))
    difference = weight_difference(student_weight, teacher_weight, column_max) * 2.0**15
    coded = difference.astype(jnp.float16)

    far = flip(coded, 4)
    near = flip(coded, 2)
    far, near, peers[0], near_keep = together(far, near, peers[0], near_keep)
    across = [flip(far[:, half], 2) for half in halves]
    peers[1], across[0] = together(peers[1], across[0])
    pieces = [(keep,), (near_keep,), peers, [swap_cores(peer) for peer in peers]]

    def residual(c):
        parts = [p[:, halves[c]].astype(f32) for p in (difference, near, far)]
        pairs = [high_low(p) for p in (*parts, across[c].astype(f32))]
        return partial_residual(pieces, [p[0] for p in pairs], [p[1] for p in pairs])

    mine, sent = residual(0)
    theirs = flip(sent, 1)
    mine_next, sent_next = residual(1)
    theirs_next = flip(sent_next, 1)

    loss = jnp.zeros((1, columns), f32)
    loss, own, rest, to_across, to_near = partial_gradient(
        pieces, mine, theirs, loss, total_tokens, False
    )
    from_across = flip(to_across, 2)
    theirs_next, from_across = together(theirs_next, from_across)
    loss_next, own_next, rest_next, to_across, to_near_next = partial_gradient(
        pieces, mine_next, theirs_next, loss, total_tokens, True
    )
    from_near = flip(to_near, 2)
    from_across, from_near, to_across = together(from_across, from_near, to_across)
    from_across_next = flip(to_across, 2)
    to_far, _ = join_far(rest, from_across, loss)
    from_far = flip(to_far, 4)
    states = (student_weight, first_moment, second_moment)
    news = apply_update(0, own, from_near, from_far, states)
    to_far, loss = join_far(rest_next, from_across_next, loss_next)
    from_far_next = flip(to_far, 4)
    from_near_next = flip(to_near_next, 2)
    from_far_next, *news = together(from_far_next, *news)
    loss = total_loss(loss, from_far_next, total_tokens)
    loss = jnp.sum(loss + swap_cores(loss)).reshape(1)
    news = apply_update(1, own_next, from_near_next, from_far_next, states, news)
    return (*news, loss)


def solution(mesh):
    fsdp, tensor = mesh.shape["fsdp"], mesh.shape["tensor"]

    def per_device(hidden_states, *weights):
        rows = weights[0].shape[0]
        few = fsdp == 8 and tensor == 2 and rows % 128 == 0 and weights[0].shape[1] % 256 == 0
        return (paired if few else generic)(hidden_states, *weights)

    rows = P(("groups", "fsdp"), "tensor")
    in_specs = (P(("groups", "fsdp", "tensor"), None), P("fsdp", "tensor"), rows, rows, rows)
    out_specs = (rows, rows, rows, P("groups"))
    return jax.shard_map(
        per_device, mesh=mesh, in_specs=in_specs, out_specs=out_specs, check_vma=False
    )
```
